32 devices in a mesh: groups: 2 (over y), tm: 4 (over z), head: 2 (over x), batch: 2 (over core).
Axes of the slice: x: 2, y: 2, z: 4, core: 2. Of those that a mesh axis runs over, the one named last changes fastest.
Arguments:
- u_input: bfloat16 [4, 1024, 1536], P(('groups', 'batch'), 'tm'), parts along dimension 0, may hold values from -6 to 6
- head_values: bfloat16 [4, 1024, 3072], P(('groups', 'batch'), 'tm', 'head'), parts along dimension 0, may hold values from -6 to 6
- grad_output: bfloat16 [4, 1024, 3072], P(('groups', 'batch'), 'tm', 'head'), parts along dimension 0, may hold values from -6 to 6
- w_bc: bfloat16 [1536, 256], replicated, may hold values from -0.15625 to 0.15625
- w_dt: bfloat16 [1536, 48], P(None, 'head'), may hold values from -0.15625 to 0.15625
- dt_bias: float32 [48], P('head'), may hold values from -1.5 to 0.5
- a_log: float32 [48], P('head'), as said below
Outputs:
- grad_input: bfloat16 [4, 1024, 1536], P(('groups', 'batch'), 'tm'), parts along dimension 0
- grad_values: bfloat16 [4, 1024, 3072], P(('groups', 'batch'), 'tm', 'head'), parts along dimension 0
- grad_w_bc: float32 [3072, 256], P(('groups', 'tm', 'batch')), parts along dimension 0
- grad_w_dt: float32 [3072, 48], P('groups', 'head'), parts along dimension 0
- grad_dt_bias: float32 [96], P(('groups', 'head')), parts along dimension 0
- grad_a_log: float32 [96], P(('groups', 'head')), parts along dimension 0
The draws below stay inside these ranges and needn't reach their ends.
There are 2 independent parts, one for each index of `groups`. The reference program is written for one: setup_inputs(seed, part) draws one part's arguments, and reference() takes and returns one part's arrays. A program takes and returns all parts, laid end to end along the dimension named above; an argument that names none is the same for every part. Nothing has to cross between parts.
Inputs may be any that keep to these rules, and one draw needn't show every extreme that they name: a_log lies between log(0.3 / 1024) and log(0.08).
All inputs are finite; a program needn't handle non-finite values.
Results may differ from the reference program's by a relative error of at most 0.0059.
Values may be sent and summed in bfloat16 or wider, within the bound.
A program may use at most 64 MiB of HBM per device.

```python
import math
import jax
import jax.numpy as jnp
from jax import lax

D = 1536
HEADS = 48
HEAD_DIM = 64
STATE = 128
TOK_DEV = 256
LENGTH = 1024
SEQS = 2
N_TM = 4


def draw_a_log(key, part):
    length_all = TOK_DEV * N_TM
    lowest = math.log(1.0 / length_all)
    highest = math.log(0.08)
    return jax.random.uniform(key, (HEADS,), jnp.float32, lowest, highest)


def block_levels(rng, shape, split, low, largest):
    def one(dim, shards_of):
        draws = jax.random.uniform(jax.random.fold_in(jax.random.fold_in(rng, 6), dim), (shards_of,), jnp.float32, low / len(split), largest / len(split))
        return jnp.repeat(jnp.exp(draws), shape[dim] // shards_of).reshape((-1,) + (1,) * (len(shape) - dim - 1))

    gain = one(*split[0])
    for cut in split[1:]:
        gain = gain * one(*cut)
    return gain


def noise(stream_key, shape, deviation, reach, cuts=(), dtype=jnp.bfloat16):
    factor_of = block_levels(stream_key, shape, cuts, -0.22, 0.18) if cuts else 1.0
    drawn = jax.random.normal(stream_key, shape, jnp.float32) * deviation * factor_of
    return jnp.minimum(jnp.maximum(drawn, -reach), reach).astype(dtype)


def setup_inputs(seed: int = 0, part: int = 0) -> dict:
    keys = jax.random.split(jax.random.key(seed), 8)
    part_keys = jax.random.split(jax.random.fold_in(keys[7], part), 8)
    u_input = noise(part_keys[0], (SEQS, LENGTH, D), 1.0, 6.0, ((0, 2), (1, 4)))
    head_values = noise(part_keys[1], (SEQS, LENGTH, HEADS * HEAD_DIM), 1.0, 6.0, ((0, 2), (1, 4), (2, 2)))
    grad_output = noise(part_keys[2], (SEQS, LENGTH, HEADS * HEAD_DIM), 1.0, 6.0, ((0, 2), (1, 4), (2, 2)))
    w_bc = noise(keys[3], (D, 2 * STATE), D ** -0.5, 0.15625)
    w_dt = noise(keys[4], (D, HEADS), D ** -0.5, 0.15625, ((1, 2),))
    dt_bias = jnp.clip(-1.5 + 2.0 * jax.random.uniform(keys[5], (HEADS,), jnp.float32) ** block_levels(keys[5], (HEADS,), ((0, 2),), -0.2, 0.2), -1.5, 0.5)
    a_log = draw_a_log(jax.random.fold_in(keys[7], 71), part)
    return dict(u_input=u_input, head_values=head_values, grad_output=grad_output, w_bc=w_bc, w_dt=w_dt, dt_bias=dt_bias, a_log=a_log)


def span_core(b_rows, c_rows, time_step, values_in, rate, state_in):
    highest = lax.Precision.HIGHEST
    log_decay = jnp.cumsum(time_step * rate[None, :], axis=0)
    length_t = time_step.shape[0]
    causal = jnp.arange(length_t)[:, None] >= jnp.arange(length_t)[None, :]
    differ = log_decay.T[:, :, None] - log_decay.T[:, None, :]
    decay = jnp.exp(jnp.where(causal[None], differ, -jnp.inf))
    scores = jnp.dot(c_rows, b_rows.T, precision=highest)
    mixing = decay * scores[None] * time_step.T[:, None, :]
    inner = jnp.einsum('hts,shp->thp', mixing, values_in, precision=highest)
    carried = jnp.exp(log_decay)[:, :, None] * jnp.einsum('tn,hpn->thp', c_rows, state_in, precision=highest)
    output = inner + carried
    tail_w = jnp.exp(log_decay[-1][None, :] - log_decay) * time_step
    final = jnp.exp(log_decay[-1])[:, None, None] * state_in + jnp.einsum('sh,shp,sn->hpn', tail_w, values_in, b_rows, precision=highest)
    return (output, final)

def sequence_forward(b_rows, c_rows, time_step, values_in, rate):

    def advance(state_in, pieces):
        output, final = span_core(pieces[0], pieces[1], pieces[2], pieces[3], rate, state_in)
        return (final, output)
    start = jnp.zeros((HEADS, HEAD_DIM, STATE), jnp.float32)
    blocks = (b_rows.reshape(N_TM, TOK_DEV, STATE), c_rows.reshape(N_TM, TOK_DEV, STATE), time_step.reshape(N_TM, TOK_DEV, HEADS), values_in.reshape(N_TM, TOK_DEV, HEADS, HEAD_DIM))
    _, outputs = lax.scan(advance, start, blocks)
    return outputs.reshape(LENGTH, HEADS, HEAD_DIM)

def reference(u_input, head_values, grad_output, w_bc, w_dt, dt_bias, a_log):
    rate = -jnp.exp(a_log)
    flat = u_input.reshape(SEQS * LENGTH, D)
    proj = jnp.dot(flat, w_bc, preferred_element_type=jnp.float32).astype(jnp.bfloat16)
    pre = jnp.dot(flat, w_dt, preferred_element_type=jnp.float32) + dt_bias[None, :]
    delta = jax.nn.softplus(pre).reshape(SEQS, LENGTH, HEADS)
    b_all = proj[:, :STATE].astype(jnp.float32).reshape(SEQS, LENGTH, STATE)
    c_all = proj[:, STATE:].astype(jnp.float32).reshape(SEQS, LENGTH, STATE)
    values_all = head_values.astype(jnp.float32).reshape(SEQS, LENGTH, HEADS, HEAD_DIM)
    cotangent = grad_output.astype(jnp.float32).reshape(SEQS, LENGTH, HEADS, HEAD_DIM)
    grad_b_list = []
    grad_c_list = []
    grad_delta_list = []
    grad_x_list = []
    rate_total = jnp.zeros((HEADS,), jnp.float32)
    for seq_index in range(SEQS):
        _, pull_back = jax.vjp(sequence_forward, b_all[seq_index], c_all[seq_index], delta[seq_index], values_all[seq_index], rate)
        g_b, g_c, g_delta, g_x, g_rate = pull_back(cotangent[seq_index])
        grad_b_list.append(g_b)
        grad_c_list.append(g_c)
        grad_delta_list.append(g_delta)
        grad_x_list.append(g_x)
        rate_total = rate_total + g_rate
    grad_proj = jnp.concatenate([jnp.stack(grad_b_list), jnp.stack(grad_c_list)], axis=-1)
    grad_proj = grad_proj.reshape(SEQS * LENGTH, 2 * STATE).astype(jnp.bfloat16)
    grad_pre = jnp.stack(grad_delta_list).reshape(SEQS * LENGTH, HEADS) * jax.nn.sigmoid(pre)
    grad_pre_b = grad_pre.astype(jnp.bfloat16)
    grad_input = (jnp.dot(grad_proj, w_bc.T, preferred_element_type=jnp.float32) + jnp.dot(grad_pre_b, w_dt.T, preferred_element_type=jnp.float32)).astype(jnp.bfloat16)
    grad_values = jnp.stack(grad_x_list).reshape(SEQS, LENGTH, HEADS * HEAD_DIM).astype(jnp.bfloat16)
    grad_w_bc = jnp.dot(flat.T, grad_proj, preferred_element_type=jnp.float32)
    grad_w_dt = jnp.dot(flat.T, grad_pre_b, preferred_element_type=jnp.float32)
    grad_dt_bias = lax.optimization_barrier(jnp.sum(grad_pre, axis=0))
    return (grad_input.reshape(SEQS, LENGTH, D), grad_values, grad_w_bc, grad_w_dt, grad_dt_bias, rate_total * rate)
```

```python
import functools

import jax
import jax.numpy as jnp
from jax import lax
from jax.experimental import pallas as pl
from jax.experimental.pallas import tpu as pltpu
from jax.sharding import PartitionSpec as P

MESH = pl.DeviceIdType.MESH
F32 = jnp.float32
BF16 = jnp.bfloat16
LANES = 128
NT = (((1,), (1,)), ((), ()))
TN = (((0,), (0,)), ((), ()))


def dot(a, b, dims=(((1,), (0,)), ((), ()))):
    return lax.dot_general(a, b, dims, preferred_element_type=F32)


def dot_exact(a, b):
    return lax.dot_general(
        a, b, (((1,), (0,)), ((), ())),
        precision=lax.Precision.HIGHEST, preferred_element_type=F32,
    )


def kernel(
    zn, hn, bn, heads, split,
    u, x, g, wbc, wdt, bias, alog,
    gin, gval, gwbc, gwdt, gsmall,
    wpad, rows, proj, l_t, l_sel, d_sel, xs, gs, own_f, own_b, gxi, st, dst, col_e, erows,
    direct, qd, gl, fin, gacc,
    sf, rf, sb, rb, wx, px, gpx, csend, crecv, plocal, zsend, zrecv, fsend, frecv,
    wsend, wrecv, wsum, wzsend, wzrecv, wfsend, wfrecv, smsend, smrecv, smzsend, smzrecv,
    f_ss, f_rs, b_ss, b_rs, h_ss, h_rs, c_ss, c_rs, z_ss, z_rs,
):
    z, hx, bt = lax.axis_index("tm"), lax.axis_index("head"), lax.axis_index("batch")
    tokens, width = u.shape
    pairs = heads // 2
    per = 2 if pairs % 2 == 0 else 1
    chunks = pairs // per
    stride = 2
    state = LANES
    rpad = wx.shape[1]
    half = width // bn
    lane = lax.broadcasted_iota(jnp.int32, (tokens, LANES), 1)
    lane1 = lax.broadcasted_iota(jnp.int32, (1, LANES), 1)
    low = lane < 64
    low1 = lane1 < 64

    barrier = pltpu.get_barrier_semaphore()
    for k in range(1, zn):
        pl.semaphore_signal(barrier, inc=1, device_id={"tm": lax.rem(z + k, zn)}, device_id_type=MESH)
    for k in range(1, hn):
        pl.semaphore_signal(barrier, inc=1, device_id={"head": lax.rem(hx + k, hn)}, device_id_type=MESH)
    for k in range(1, bn):
        pl.semaphore_signal(barrier, inc=1, device_id={"batch": lax.rem(bt + k, bn)}, device_id_type=MESH)

    wpad[...] = jnp.zeros_like(wpad)
    wpad[:, :heads] = wdt[...]
    rows[...] = jnp.zeros_like(rows)
    rows[0:1, :heads] = bias[...]
    rows[1:2, :heads] = alog[...]
    uu = u[...]
    proj[...] = dot(uu, wbc[...]).astype(BF16)
    pre = dot(uu, wpad[...]) + rows[0:1, :]
    delta = jnp.maximum(pre, 0.0) + jnp.log1p(jnp.exp(-jnp.abs(pre)))
    rate = -jnp.exp(rows[1:2, :])
    ti = lax.broadcasted_iota(jnp.int32, (tokens, tokens), 0)
    si = lax.broadcasted_iota(jnp.int32, (tokens, tokens), 1)
    log_decay = dot_exact((ti >= si).astype(F32), delta * rate)
    l_rows = log_decay.T
    for h in range(heads):
        l_t[h] = l_rows[h:h + 1, :]
    b_all, c_all = proj[:, :state], proj[:, state:]
    b_t = b_all.astype(F32).T.astype(BF16)
    c_t = c_all.astype(F32).T.astype(BF16)
    st[...] = jnp.where(ti <= si, dot(b_all, c_all, NT), 0.0)
    ident = (
        lax.broadcasted_iota(jnp.int32, (rpad, LANES), 0)
        == lax.broadcasted_iota(jnp.int32, (rpad, LANES), 1)
    ).astype(BF16)
    wx[hx] = dot(ident, wpad[...], NT).astype(BF16)

    def pick(value, head):
        return jnp.sum(jnp.where(lane == head, value, 0.0), axis=1, keepdims=True)

    def summarize(p, carry):
        cols = pl.ds(pl.multiple_of(p * LANES, LANES), LANES)
        ls = jnp.where(low, pick(log_decay, 2 * p), pick(log_decay, 2 * p + 1))
        ds = jnp.where(low, pick(delta, 2 * p), pick(delta, 2 * p + 1))
        l_sel[p] = ls
        d_sel[p] = ds
        xv = (jnp.exp(ls[tokens - 1:tokens, :] - ls) * ds * x[:, cols].astype(F32)).astype(BF16)
        gv = (jnp.exp(ls) * g[:, cols].astype(F32)).astype(BF16)
        xs[p] = xv
        gs[p] = gv
        own_f[p] = dot(b_t, xv)
        own_b[p] = dot(c_t, gv)
        return carry

    lax.fori_loop(0, pairs, summarize, 0)

    dst[...] = jnp.zeros_like(dst)
    erows[...] = jnp.zeros_like(erows)
    direct[...] = jnp.zeros_like(direct)
    qd[...] = jnp.zeros_like(qd)
    gl[...] = jnp.zeros_like(gl)
    fin[...] = jnp.zeros_like(fin)
    gacc[...] = jnp.zeros_like(gacc)

    @pl.when(z == 0)
    def _():
        rf[...] = jnp.zeros_like(rf)

    @pl.when(z == zn - 1)
    def _():
        rb[...] = jnp.zeros_like(rb)

    pl.semaphore_wait(barrier, zn + hn + bn - 3)

    def head_copies(k):
        to = {"head": lax.rem(hx + k, hn)}
        return [
            pltpu.make_async_remote_copy(
                ref.at[hx], ref.at[hx], h_ss.at[i, k], h_rs.at[i, k], device_id=to, device_id_type=MESH
            )
            for i, ref in enumerate((wx, px, gpx))
        ]

    for k in range(1, hn):
        head_copies(k)[0].start()

    def chain_f(c):
        part = pl.ds(c * per, per)
        return pltpu.make_async_remote_copy(
            sf.at[part], rf.at[part], f_ss.at[c], f_rs.at[c],
            device_id={"tm": lax.rem(z + 1, zn)}, device_id_type=MESH,
        )

    def chain_b(c):
        part = pl.ds(c * per, per)
        return pltpu.make_async_remote_copy(
            sb.at[part], rb.at[part], b_ss.at[c], b_rs.at[c],
            device_id={"tm": lax.rem(z + zn - 1, zn)}, device_id_type=MESH,
        )

    def chain_step(c, first, last, make, own, send, recv):
        @pl.when((c >= 0) & (c < chunks))
        def _():
            @pl.when(jnp.logical_not(first))
            def _():
                make(c).wait_recv()

            @pl.when(jnp.logical_not(last))
            def _():
                for j in range(per):
                    p = c * per + j
                    total = jnp.exp(l_sel[p, tokens - 1:tokens, :])
                    send[p] = (total * recv[p].astype(F32) + own[p]).astype(BF16)
                make(c).start()

    lm = low.astype(F32).astype(BF16)

    def local_pair(p):
        cols = pl.ds(pl.multiple_of(p * LANES, LANES), LANES)
        gb = g[:, cols]
        xb = x[:, cols]
        sh = tokens // 2
        for s0 in (0, sh):
            t0 = s0
            gx = []
            gt = gb[t0:, :]
            sm = st[s0:s0 + sh, t0:]
            add = jnp.zeros((sh, tokens - t0), F32)
            zero = [jnp.zeros((1, t0), F32)] if t0 else []
            dr = direct[s0:s0 + sh, :]
            for j in range(2):
                keep = lm[s0:s0 + sh, :]
                xm = xb[s0:s0 + sh, :] * (keep if j == 0 else (1.0 - keep).astype(BF16))
                dm = dot(xm, gt, NT)
                lc = l_sel[p, s0:s0 + sh, 64 * j:64 * j + 1]
                dc = d_sel[p, s0:s0 + sh, 64 * j:64 * j + 1]
                lr = l_t[2 * p + j][:, t0:]
                decay = jnp.exp(jnp.minimum(lr - lc, 0.0))
                gx.append(dot((decay * sm).astype(BF16), gt))
                dmd = dm * decay
                add = add + dmd * dc
                w = dmd * sm
                dr = dr + jnp.where(lane[:sh] == 2 * p + j, jnp.sum(w, axis=1, keepdims=True), 0.0)
                ce = jnp.concatenate(zero + [jnp.sum(w * dc, axis=0, keepdims=True)], axis=1)
                col_e[2 * p + j] = ce if s0 == 0 else col_e[2 * p + j] + ce
            direct[s0:s0 + sh, :] = dr
            dst[s0:s0 + sh, t0:] += add
            gxi[p, s0:s0 + sh, :] = jnp.where(low[:sh], gx[0], gx[1])

    def mixed(i, carry):
        chain_step(i - z * stride, z == 0, z == zn - 1, chain_f, own_f, sf, rf)
        chain_step(i - (zn - 1 - z) * stride, z == zn - 1, z == 0, chain_b, own_b, sb, rb)

        @pl.when(i < pairs)
        def _():
            local_pair(i)

        return carry

    lax.fori_loop(0, max(pairs, (zn - 1) * stride + chunks), mixed, 0)

    def carried(p, carry):
        cols = pl.ds(pl.multiple_of(p * LANES, LANES), LANES)
        entering, leaving = rf[p], rb[p]
        ls, ds = l_sel[p], d_sel[p]
        last = ls[tokens - 1:tokens, :]
        car = jnp.exp(ls) * g[:, cols].astype(F32) * dot(c_all, entering)
        br = jnp.exp(last - ls) * dot(b_all, leaving)
        gval[:, cols] = (ds * (gxi[p] + br)).astype(BF16)
        q = x[:, cols].astype(F32) * br
        ends = jnp.exp(last) * jnp.sum(entering.astype(F32) * leaving.astype(F32), axis=0, keepdims=True)
        q_new, c_new, e_new = qd[...], gl[...], fin[...]
        for j in range(2):
            mine, mine1 = (low, low1) if j == 0 else (~low, ~low1)
            at, at1 = lane == 2 * p + j, lane1 == 2 * p + j
            q_new = q_new + jnp.where(at, jnp.sum(jnp.where(mine, q, 0.0), axis=1, keepdims=True), 0.0)
            c_new = c_new + jnp.where(at, jnp.sum(jnp.where(mine, car, 0.0), axis=1, keepdims=True), 0.0)
            e_new = e_new + jnp.where(at1, jnp.sum(jnp.where(mine1, ends, 0.0), axis=1, keepdims=True), 0.0)
        qd[...], gl[...], fin[...] = q_new, c_new, e_new
        gacc[:, :state] += dot(xs[p], leaving, NT)
        gacc[:, state:] += dot(gs[p], entering, NT)
        return carry

    lax.fori_loop(0, pairs, carried, 0)

    d_masked = jnp.where(ti <= si, dst[...], 0.0).astype(BF16)
    px[hx, :, :state] = (gacc[:, :state] + dot(d_masked, c_all)).astype(BF16)
    px[hx, :, state:] = (gacc[:, state:] + dot(d_masked, b_all, TN)).astype(BF16)
    for k in range(1, hn):
        head_copies(k)[1].start()

    q_all = qd[...]
    straight = direct[...] + q_all
    for h in range(heads):
        erows[h:h + 1, :] = col_e[h]
    g_log = gl[...] + erows[...].T - delta * straight
    tail = jnp.sum(delta * q_all, axis=0, keepdims=True) + fin[...]
    back = dot_exact((ti <= si).astype(F32), g_log) + tail
    g_delta = straight + rate * back
    g_pre = g_delta * jax.nn.sigmoid(pre)
    smsend[...] = jnp.zeros_like(smsend)
    smsend[0:1, :] = jnp.sum(g_pre, axis=0, keepdims=True)
    smsend[1:2, :] = jnp.sum(delta * back, axis=0, keepdims=True) * rate
    gpx[hx] = g_pre.T[:rpad, :].astype(BF16)
    for k in range(1, hn):
        head_copies(k)[2].start()
    wsend[...] = dot(gpx[hx], uu).astype(BF16)

    other = {"batch": lax.rem(bt + 1, bn)}

    def core_copy(i, src, to):
        return pltpu.make_async_remote_copy(src, to, c_ss.at[i], c_rs.at[i], device_id=other, device_id_type=MESH)

    core_w = core_copy(0, wsend, wrecv)
    core_s = core_copy(1, smsend, smrecv)
    core_p = core_copy(2, csend, crecv)
    core_f = core_copy(3, wfsend, wfrecv)
    core_w.start()
    core_s.start()

    def along(i, src, to, k):
        there = lax.rem(z + k, zn)
        return pltpu.make_async_remote_copy(
            src, to.at[z], z_ss.at[i, k], z_rs.at[i, k], device_id={"tm": there}, device_id_type=MESH
        )

    def each_z(body):
        def turn(k, carry):
            body(k)
            return carry

        lax.fori_loop(1, zn, turn, 0)

    def z_start_small(k):
        along(0, wzsend, wzrecv, k).start()
        along(1, smzsend, smzrecv, k).start()

    def z_start_large(k):
        along(2, zsend.at[lax.rem(z + k, zn)], zrecv, k).start()

    def z_wait_small(k):
        along(0, wzsend, wzrecv, k).wait()
        along(1, smzsend, smzrecv, k).wait()

    def z_wait_large(k):
        along(2, zsend.at[lax.rem(z + k, zn)], zrecv, k).wait()

    for k in range(1, hn):
        for copy in head_copies(k):
            copy.wait()
    gp = px[0].astype(F32)
    for k in range(1, hn):
        gp = gp + px[k].astype(F32)
    gp = gp.astype(BF16)
    wide = zrecv.shape[2]
    if split:
        piece = jnp.where(hx == 0, gp[:, :wide], gp[:, wide:])
    else:
        piece = gp
    block = zrecv.shape[1]
    local = dot(uu, piece, TN)
    for k in range(zn * bn):
        plocal[k] = local[k * block:(k + 1) * block, :]
    for k in range(zn):
        csend[k] = plocal[k * bn + lax.rem(bt + 1, bn)].astype(BF16)
    core_p.start()

    core_w.wait()
    core_s.wait()
    wsum[...] = wsend[...].astype(F32) + wrecv[...].astype(F32)
    mine = pl.ds(pl.multiple_of(bt * half, LANES), half)
    theirs = pl.ds(pl.multiple_of(lax.rem(bt + 1, bn) * half, LANES), half)
    wz = wsum[:, mine].astype(BF16)
    wzsend[...] = wz
    wzrecv[z] = wz
    sz = smsend[...] + smrecv[...]
    smzsend[...] = sz
    smzrecv[z] = sz
    each_z(z_start_small)

    core_p.wait()
    for k in range(zn):
        zsend[k] = (plocal[k * bn + bt] + crecv[k].astype(F32)).astype(BF16)
    zrecv[z] = zsend[z]
    each_z(z_start_large)

    gpa = gpx[...].reshape(hn * rpad, tokens).astype(F32).T.astype(BF16)
    wa = wx[...].reshape(hn * rpad, width)
    gin[...] = (dot(gp, wbc[...], NT) + dot(gpa, wa)).astype(BF16)

    each_z(z_wait_small)
    total_w = wzrecv[0].astype(F32)
    total_s = smzrecv[0]
    for k in range(1, zn):
        total_w = total_w + wzrecv[k].astype(F32)
        total_s = total_s + smzrecv[k]
    wfsend[...] = total_w
    core_f.start()
    gsmall[...] = total_s
    gwdt[:, mine] = total_w

    each_z(z_wait_large)
    total = zrecv[0].astype(F32)
    for k in range(1, zn):
        total = total + zrecv[k].astype(F32)
    if split:
        fsend[...] = total
        final = pltpu.make_async_remote_copy(
            fsend, frecv, c_ss.at[4], c_rs.at[4], device_id={"head": lax.rem(hx + 1, hn)}, device_id_type=MESH
        )
        final.start()
        gwbc[:, pl.ds(pl.multiple_of(hx * wide, LANES), wide)] = total
        final.wait()
        gwbc[:, pl.ds(pl.multiple_of((1 - hx) * wide, LANES), wide)] = frecv[...]
    else:
        gwbc[...] = total
    core_f.wait()
    gwdt[:, theirs] = wfrecv[...]

    def drain(c, carry):
        @pl.when(z < zn - 1)
        def _():
            chain_f(c).wait_send()

        @pl.when(z > 0)
        def _():
            chain_b(c).wait_send()

        return carry

    lax.fori_loop(0, chunks, drain, 0)


def on_device(sizes, u_input, head_values, grad_output, w_bc, w_dt, dt_bias, a_log):
    zn, hn, bn = sizes
    seqs, tokens, width = u_input.shape
    assert seqs == 1 and bn == 2
    heads = w_dt.shape[1]
    values = head_values.shape[2]
    both = w_bc.shape[1]
    pairs = heads // 2
    assert values == heads * 64 and both == 2 * LANES and heads % 2 == 0
    split = hn == 2
    wide = both // 2 if split else both
    block = width // (zn * bn)
    rpad = -(-heads // 16) * 16
    half = width // bn
    chunks = pairs // 2 if pairs % 2 == 0 else pairs
    vm = pltpu.VMEM
    dma = pltpu.SemaphoreType.DMA
    scratch = [
        vm((width, LANES), BF16), vm((8, LANES), F32), vm((tokens, both), BF16), vm((heads, 1, tokens), F32),
        vm((pairs, tokens, LANES), F32), vm((pairs, tokens, LANES), F32),
        vm((pairs, tokens, LANES), BF16), vm((pairs, tokens, LANES), BF16),
        vm((pairs, LANES, LANES), F32), vm((pairs, LANES, LANES), F32), vm((pairs, tokens, LANES), F32),
        vm((tokens, tokens), F32), vm((tokens, tokens), F32), vm((heads, 1, tokens), F32), vm((LANES, tokens), F32),
        vm((tokens, LANES), F32), vm((tokens, LANES), F32), vm((tokens, LANES), F32), vm((1, LANES), F32),
        vm((tokens, both), F32),
        vm((pairs, LANES, LANES), BF16), vm((pairs, LANES, LANES), BF16),
        vm((pairs, LANES, LANES), BF16), vm((pairs, LANES, LANES), BF16),
        vm((hn, rpad, width), BF16), vm((hn, tokens, both), BF16), vm((hn, rpad, tokens), BF16),
        vm((zn, block, wide), BF16), vm((zn, block, wide), BF16), vm((zn * bn, block, wide), F32),
        vm((zn, block, wide), BF16), vm((zn, block, wide), BF16), vm((block, wide), F32), vm((block, wide), F32),
        vm((rpad, width), BF16), vm((rpad, width), BF16), vm((rpad, width), F32),
        vm((rpad, half), BF16), vm((zn, rpad, half), BF16), vm((rpad, half), F32), vm((rpad, half), F32),
        vm((8, LANES), F32), vm((8, LANES), F32), vm((8, LANES), F32), vm((zn, 8, LANES), F32),
        dma((chunks,)), dma((chunks,)), dma((chunks,)), dma((chunks,)),
        dma((3, hn)), dma((3, hn)), dma((5,)), dma((5,)), dma((3, zn)), dma((3, zn)),
    ]
    spec = pl.BlockSpec(memory_space=pltpu.VMEM)
    gin, gval, gwbc, gwdt, small = pl.pallas_call(
        functools.partial(kernel, zn, hn, bn, heads, split),
        out_shape=(
            jax.ShapeDtypeStruct((tokens, width), BF16),
            jax.ShapeDtypeStruct((tokens, values), BF16),
            jax.ShapeDtypeStruct((block, both), F32),
            jax.ShapeDtypeStruct((rpad, width), F32),
            jax.ShapeDtypeStruct((8, LANES), F32),
        ),
        in_specs=[spec] * 7,
        out_specs=[spec] * 5,
        scratch_shapes=scratch,
        compiler_params=pltpu.CompilerParams(
            collective_id=0, has_side_effects=True, vmem_limit_bytes=56 << 20
        ),
    )(
        u_input.reshape(tokens, width), head_values.reshape(tokens, values), grad_output.reshape(tokens, values),
        w_bc, w_dt, dt_bias.reshape(1, heads), a_log.reshape(1, heads),
    )
    return (
        gin.reshape(1, tokens, width), gval.reshape(1, tokens, values), gwbc,
        gwdt[:heads].T, small[0, :heads], small[1, :heads],
    )


def solution(mesh):
    sizes = (mesh.shape["tm"], mesh.shape["head"], mesh.shape["batch"])
    return jax.shard_map(
        functools.partial(on_device, sizes),
        mesh=mesh,
        in_specs=(
            P(("groups", "batch"), "tm", None),
            P(("groups", "batch"), "tm", "head"),
            P(("groups", "batch"), "tm", "head"),
            P(),
            P(None, "head"),
            P("head"),
            P("head"),
        ),
        out_specs=(
            P(("groups", "batch"), "tm", None),
            P(("groups", "batch"), "tm", "head"),
            P(("groups", "tm", "batch"), None),
            P("groups", "head"),
            P(("groups", "head")),
            P(("groups", "head")),
        ),
        check_vma=False,
    )
```

```python
import functools

import jax
import jax.numpy as jnp
from jax import lax
from jax.experimental import pallas as pl
from jax.experimental.pallas import tpu as pltpu
from jax.sharding import PartitionSpec as P

MESH = pl.DeviceIdType.MESH
F32 = jnp.float32
BF16 = jnp.bfloat16
LANES = 128
NT = (((1,), (1,)), ((), ()))
TN = (((0,), (0,)), ((), ()))


def dot(a, b, dims=(((1,), (0,)), ((), ()))):
    return lax.dot_general(a, b, dims, preferred_element_type=F32)


def dot_exact(a, b):
    return lax.dot_general(
        a, b, (((1,), (0,)), ((), ())),
        precision=lax.Precision.HIGHEST, preferred_element_type=F32,
    )


def kernel(
    zn, hn, bn, heads, split,
    u, x, g, wbc, wdt, bias, alog,
    gin, gval, gwbc, gwdt, gbias, galog,
    wpad, ut, rows, proj, l_t, l_sel, d_sel, xs, gs, own_f, own_b, gxi, st, dst, col_e, erows,
    direct, qd, gl, fin, gacc,
    sf, rf, sb, rb, wx, px, gpx, csend, crecv, plocal, zsend, zrecv, fsend, frecv,
    wsend, wrecv, wsum, wzsend, wzrecv, wfsend, wfrecv, smsend, smrecv, smzsend, smzrecv,
    f_ss, f_rs, b_ss, b_rs, h_ss, h_rs, c_ss, c_rs, z_ss, z_rs,
):
    z, hx, bt = lax.axis_index("tm"), lax.axis_index("head"), lax.axis_index("batch")
    tokens, width = u.shape
    pairs = heads // 2
    per = 2 if pairs % 2 == 0 else 1
    chunks = pairs // per
    stride = 2
    state = LANES
    rpad = wx.shape[1]
    half = width // bn
    lane = lax.broadcasted_iota(jnp.int32, (tokens, LANES), 1)
    lane1 = lax.broadcasted_iota(jnp.int32, (1, LANES), 1)
    low = lane < 64
    low1 = lane1 < 64

    barrier = pltpu.get_barrier_semaphore()
    for k in range(1, zn):
        pl.semaphore_signal(barrier, inc=1, device_id={"tm": lax.rem(z + k, zn)}, device_id_type=MESH)
    for k in range(1, hn):
        pl.semaphore_signal(barrier, inc=1, device_id={"head": lax.rem(hx + k, hn)}, device_id_type=MESH)
    for k in range(1, bn):
        pl.semaphore_signal(barrier, inc=1, device_id={"batch": lax.rem(bt + k, bn)}, device_id_type=MESH)

    wpad[...] = jnp.zeros_like(wpad)
    wpad[:heads, :] = wdt[...]
    rows[...] = jnp.zeros_like(rows)
    rows[0:1, :heads] = bias[...]
    rows[1:2, :heads] = alog[...]
    uu = u[...]
    proj[...] = dot(uu, wbc[...]).astype(BF16)
    pre = dot(uu, wpad[...], NT) + rows[0:1, :]
    delta = jnp.maximum(pre, 0.0) + jnp.log1p(jnp.exp(-jnp.abs(pre)))
    rate = -jnp.exp(rows[1:2, :])
    ti = lax.broadcasted_iota(jnp.int32, (tokens, tokens), 0)
    si = lax.broadcasted_iota(jnp.int32, (tokens, tokens), 1)
    log_decay = dot_exact((ti >= si).astype(F32), delta * rate)
    l_rows = log_decay.T
    for h in range(heads):
        l_t[h] = l_rows[h:h + 1, :]
    b_all, c_all = proj[:, :state], proj[:, state:]
    b_t = b_all.astype(F32).T.astype(BF16)
    c_t = c_all.astype(F32).T.astype(BF16)
    st[...] = jnp.where(ti <= si, dot(b_all, c_all, NT), 0.0)
    wx[hx] = wpad[:rpad, :]

    def pick(value, head):
        return jnp.sum(jnp.where(lane == head, value, 0.0), axis=1, keepdims=True)

    def summarize(p, carry):
        cols = pl.ds(pl.multiple_of(p * LANES, LANES), LANES)
        ls = jnp.where(low, pick(log_decay, 2 * p), pick(log_decay, 2 * p + 1))
        ds = jnp.where(low, pick(delta, 2 * p), pick(delta, 2 * p + 1))
        l_sel[p] = ls
        d_sel[p] = ds
        xv = (jnp.exp(ls[tokens - 1:tokens, :] - ls) * ds * x[:, cols].astype(F32)).astype(BF16)
        gv = (jnp.exp(ls) * g[:, cols].astype(F32)).astype(BF16)
        xs[p] = xv
        gs[p] = gv
        own_f[p] = dot(b_t, xv)
        own_b[p] = dot(c_t, gv)
        return carry

    lax.fori_loop(0, pairs, summarize, 0)

    dst[...] = jnp.zeros_like(dst)
    erows[...] = jnp.zeros_like(erows)
    direct[...] = jnp.zeros_like(direct)
    qd[...] = jnp.zeros_like(qd)
    gl[...] = jnp.zeros_like(gl)
    fin[...] = jnp.zeros_like(fin)
    gacc[...] = jnp.zeros_like(gacc)

    @pl.when(z == 0)
    def _():
        rf[...] = jnp.zeros_like(rf)

    @pl.when(z == zn - 1)
    def _():
        rb[...] = jnp.zeros_like(rb)

    pl.semaphore_wait(barrier, zn + hn + bn - 3)

    def head_copies(k):
        to = {"head": lax.rem(hx + k, hn)}
        return [
            pltpu.make_async_remote_copy(
                ref.at[hx], ref.at[hx], h_ss.at[i, k], h_rs.at[i, k], device_id=to, device_id_type=MESH
            )
            for i, ref in enumerate((wx, px, gpx))
        ]

    for k in range(1, hn):
        head_copies(k)[0].start()

    def chain_f(c):
        part = pl.ds(c * per, per)
        return pltpu.make_async_remote_copy(
            sf.at[part], rf.at[part], f_ss.at[c], f_rs.at[c],
            device_id={"tm": lax.rem(z + 1, zn)}, device_id_type=MESH,
        )

    def chain_b(c):
        part = pl.ds(c * per, per)
        return pltpu.make_async_remote_copy(
            sb.at[part], rb.at[part], b_ss.at[c], b_rs.at[c],
            device_id={"tm": lax.rem(z + zn - 1, zn)}, device_id_type=MESH,
        )

    def chain_step(c, first, last, make, own, send, recv):
        @pl.when((c >= 0) & (c < chunks))
        def _():
            @pl.when(jnp.logical_not(first))
            def _():
                make(c).wait_recv()

            @pl.when(jnp.logical_not(last))
            def _():
                for j in range(per):
                    p = c * per + j
                    total = jnp.exp(l_sel[p, tokens - 1:tokens, :])
                    send[p] = (total * recv[p].astype(F32) + own[p]).astype(BF16)
                make(c).start()

    lm = low.astype(F32).astype(BF16)

    def local_pair(p):
        cols = pl.ds(pl.multiple_of(p * LANES, LANES), LANES)
        gb = g[:, cols]
        xb = x[:, cols]
        sh = tokens // 2
        for s0 in (0, sh):
            t0 = s0
            gx = []
            gt = gb[t0:, :]
            sm = st[s0:s0 + sh, t0:]
            add = jnp.zeros((sh, tokens - t0), F32)
            zero = [jnp.zeros((1, t0), F32)] if t0 else []
            dr = direct[s0:s0 + sh, :]
            for j in range(2):
                keep = lm[s0:s0 + sh, :]
                xm = xb[s0:s0 + sh, :] * (keep if j == 0 else (1.0 - keep).astype(BF16))
                dm = dot(xm, gt, NT)
                lc = l_sel[p, s0:s0 + sh, 64 * j:64 * j + 1]
                dc = d_sel[p, s0:s0 + sh, 64 * j:64 * j + 1]
                lr = l_t[2 * p + j][:, t0:]
                decay = jnp.exp(jnp.minimum(lr - lc, 0.0))
                gx.append(dot((decay * sm).astype(BF16), gt))
                dmd = dm * decay
                add = add + dmd * dc
                w = dmd * sm
                dr = dr + jnp.where(lane[:sh] == 2 * p + j, jnp.sum(w, axis=1, keepdims=True), 0.0)
                ce = jnp.concatenate(zero + [jnp.sum(w * dc, axis=0, keepdims=True)], axis=1)
                col_e[2 * p + j] = ce if s0 == 0 else col_e[2 * p + j] + ce
            direct[s0:s0 + sh, :] = dr
            dst[s0:s0 + sh, t0:] += add
            gxi[p, s0:s0 + sh, :] = jnp.where(low[:sh], gx[0], gx[1])

    def mixed(i, carry):
        chain_step(i - z * stride, z == 0, z == zn - 1, chain_f, own_f, sf, rf)
        chain_step(i - (zn - 1 - z) * stride, z == zn - 1, z == 0, chain_b, own_b, sb, rb)

        @pl.when(i < pairs)
        def _():
            local_pair(i)

        return carry

    lax.fori_loop(0, max(pairs, (zn - 1) * stride + chunks), mixed, 0)

    def carried(p, carry):
        cols = pl.ds(pl.multiple_of(p * LANES, LANES), LANES)
        entering, leaving = rf[p], rb[p]
        ls, ds = l_sel[p], d_sel[p]
        last = ls[tokens - 1:tokens, :]
        car = jnp.exp(ls) * g[:, cols].astype(F32) * dot(c_all, entering)
        br = jnp.exp(last - ls) * dot(b_all, leaving)
        gval[:, cols] = (ds * (gxi[p] + br)).astype(BF16)
        q = x[:, cols].astype(F32) * br
        ends = jnp.exp(last) * jnp.sum(entering.astype(F32) * leaving.astype(F32), axis=0, keepdims=True)
        q_new, c_new, e_new = qd[...], gl[...], fin[...]
        for j in range(2):
            mine, mine1 = (low, low1) if j == 0 else (~low, ~low1)
            at, at1 = lane == 2 * p + j, lane1 == 2 * p + j
            q_new = q_new + jnp.where(at, jnp.sum(jnp.where(mine, q, 0.0), axis=1, keepdims=True), 0.0)
            c_new = c_new + jnp.where(at, jnp.sum(jnp.where(mine, car, 0.0), axis=1, keepdims=True), 0.0)
            e_new = e_new + jnp.where(at1, jnp.sum(jnp.where(mine1, ends, 0.0), axis=1, keepdims=True), 0.0)
        qd[...], gl[...], fin[...] = q_new, c_new, e_new
        gacc[:, :state] += dot(xs[p], leaving, NT)
        gacc[:, state:] += dot(gs[p], entering, NT)
        return carry

    lax.fori_loop(0, pairs, carried, 0)

    d_masked = jnp.where(ti <= si, dst[...], 0.0).astype(BF16)
    px[hx, :, :state] = (gacc[:, :state] + dot(d_masked, c_all)).astype(BF16)
    px[hx, :, state:] = (gacc[:, state:] + dot(d_masked, b_all, TN)).astype(BF16)
    for k in range(1, hn):
        head_copies(k)[1].start()

    q_all = qd[...]
    straight = direct[...] + q_all
    for h in range(heads):
        erows[h:h + 1, :] = col_e[h]
    g_log = gl[...] + erows[...].T - delta * straight
    tail = jnp.sum(delta * q_all, axis=0, keepdims=True) + fin[...]
    back = dot_exact((ti <= si).astype(F32), g_log) + tail
    g_delta = straight + rate * back
    g_pre = g_delta * jax.nn.sigmoid(pre)
    smsend[...] = jnp.zeros_like(smsend)
    smsend[0:1, :] = jnp.sum(g_pre, axis=0, keepdims=True)
    smsend[1:2, :] = jnp.sum(delta * back, axis=0, keepdims=True) * rate
    gpx[hx] = g_pre.T[:rpad, :].astype(BF16)
    for k in range(1, hn):
        head_copies(k)[2].start()
    wsend[...] = dot(gpx[hx], uu).astype(BF16)

    other = {"batch": lax.rem(bt + 1, bn)}

    def core_copy(i, src, to):
        return pltpu.make_async_remote_copy(src, to, c_ss.at[i], c_rs.at[i], device_id=other, device_id_type=MESH)

    core_w = core_copy(0, wsend, wrecv)
    core_s = core_copy(1, smsend, smrecv)
    core_p = core_copy(2, csend, crecv)
    core_f = core_copy(3, wfsend, wfrecv)
    core_w.start()
    core_s.start()

    def along(i, src, to, k):
        there = lax.rem(z + k, zn)
        return pltpu.make_async_remote_copy(
            src, to.at[z], z_ss.at[i, k], z_rs.at[i, k], device_id={"tm": there}, device_id_type=MESH
        )

    def each_z(body):
        def turn(k, carry):
            body(k)
            return carry

        lax.fori_loop(1, zn, turn, 0)

    def z_start_small(k):
        along(0, wzsend, wzrecv, k).start()
        along(1, smzsend, smzrecv, k).start()

    def z_start_large(k):
        along(2, zsend.at[lax.rem(z + k, zn)], zrecv, k).start()

    def z_wait_small(k):
        along(0, wzsend, wzrecv, k).wait()
        along(1, smzsend, smzrecv, k).wait()

    def z_wait_large(k):
        along(2, zsend.at[lax.rem(z + k, zn)], zrecv, k).wait()

    for k in range(width // 256):
        at = k * 256
        ut[at:at + 256, :] = u[:, at:at + 256].astype(F32).T.astype(BF16)

    for k in range(1, hn):
        for copy in head_copies(k):
            copy.wait()
    gp = px[0].astype(F32)
    for k in range(1, hn):
        gp = gp + px[k].astype(F32)
    gp = gp.astype(BF16)
    wide = zrecv.shape[2]
    if split:
        piece = jnp.where(hx == 0, gp[:, :wide], gp[:, wide:])
    else:
        piece = gp
    block = zrecv.shape[1]
    local = dot(ut[...], piece)
    for k in range(zn * bn):
        plocal[k] = local[k * block:(k + 1) * block, :]
    for k in range(zn):
        csend[k] = plocal[k * bn + lax.rem(bt + 1, bn)].astype(BF16)
    core_p.start()

    core_w.wait()
    core_s.wait()
    wsum[...] = wsend[...].astype(F32) + wrecv[...].astype(F32)
    mine = pl.ds(pl.multiple_of(bt * half, LANES), half)
    theirs = pl.ds(pl.multiple_of(lax.rem(bt + 1, bn) * half, LANES), half)
    wz = wsum[:, mine].astype(BF16)
    wzsend[...] = wz
    wzrecv[z] = wz
    sz = smsend[...] + smrecv[...]
    smzsend[...] = sz
    smzrecv[z] = sz
    each_z(z_start_small)

    core_p.wait()
    for k in range(zn):
        zsend[k] = (plocal[k * bn + bt] + crecv[k].astype(F32)).astype(BF16)
    zrecv[z] = zsend[z]
    each_z(z_start_large)

    gpa = gpx[...].reshape(hn * rpad, tokens).astype(F32).T.astype(BF16)
    wa = wx[...].reshape(hn * rpad, width)
    gin[...] = (dot(gp, wbc[...], NT) + dot(gpa, wa)).astype(BF16)

    each_z(z_wait_small)
    total_w = wzrecv[0].astype(F32)
    total_s = smzrecv[0]
    for k in range(1, zn):
        total_w = total_w + wzrecv[k].astype(F32)
        total_s = total_s + smzrecv[k]
    wfsend[...] = total_w
    core_f.start()
    gbias[...] = total_s[0:1, :heads]
    galog[...] = total_s[1:2, :heads]
    gwdt[:, mine] = total_w[:heads, :]

    each_z(z_wait_large)
    total = zrecv[0].astype(F32)
    for k in range(1, zn):
        total = total + zrecv[k].astype(F32)
    if split:
        fsend[...] = total
        final = pltpu.make_async_remote_copy(
            fsend, frecv, c_ss.at[4], c_rs.at[4], device_id={"head": lax.rem(hx + 1, hn)}, device_id_type=MESH
        )
        final.start()
        gwbc[:, pl.ds(pl.multiple_of(hx * wide, LANES), wide)] = total
        final.wait()
        gwbc[:, pl.ds(pl.multiple_of((1 - hx) * wide, LANES), wide)] = frecv[...]
    else:
        gwbc[...] = total
    core_f.wait()
    gwdt[:, theirs] = wfrecv[:heads, :]

    def drain(c, carry):
        @pl.when(z < zn - 1)
        def _():
            chain_f(c).wait_send()

        @pl.when(z > 0)
        def _():
            chain_b(c).wait_send()

        return carry

    lax.fori_loop(0, chunks, drain, 0)


def on_device(sizes, u_input, head_values, grad_output, w_bc, w_dt, dt_bias, a_log):
    zn, hn, bn = sizes
    seqs, tokens, width = u_input.shape
    assert seqs == 1 and bn == 2
    heads = w_dt.shape[1]
    values = head_values.shape[2]
    both = w_bc.shape[1]
    pairs = heads // 2
    assert values == heads * 64 and both == 2 * LANES and heads % 2 == 0
    split = hn == 2
    wide = both // 2 if split else both
    block = width // (zn * bn)
    rpad = -(-heads // 16) * 16
    half = width // bn
    chunks = pairs // 2 if pairs % 2 == 0 else pairs
    vm = pltpu.VMEM
    dma = pltpu.SemaphoreType.DMA
    scratch = [
        vm((LANES, width), BF16), vm((width, tokens), BF16), vm((8, LANES), F32), vm((tokens, both), BF16), vm((heads, 1, tokens), F32),
        vm((pairs, tokens, LANES), F32), vm((pairs, tokens, LANES), F32),
        vm((pairs, tokens, LANES), BF16), vm((pairs, tokens, LANES), BF16),
        vm((pairs, LANES, LANES), F32), vm((pairs, LANES, LANES), F32), vm((pairs, tokens, LANES), F32),
        vm((tokens, tokens), F32), vm((tokens, tokens), F32), vm((heads, 1, tokens), F32), vm((LANES, tokens), F32),
        vm((tokens, LANES), F32), vm((tokens, LANES), F32), vm((tokens, LANES), F32), vm((1, LANES), F32),
        vm((tokens, both), F32),
        vm((pairs, LANES, LANES), BF16), vm((pairs, LANES, LANES), BF16),
        vm((pairs, LANES, LANES), BF16), vm((pairs, LANES, LANES), BF16),
        vm((hn, rpad, width), BF16), vm((hn, tokens, both), BF16), vm((hn, rpad, tokens), BF16),
        vm((zn, block, wide), BF16), vm((zn, block, wide), BF16), vm((zn * bn, block, wide), F32),
        vm((zn, block, wide), BF16), vm((zn, block, wide), BF16), vm((block, wide), F32), vm((block, wide), F32),
        vm((rpad, width), BF16), vm((rpad, width), BF16), vm((rpad, width), F32),
        vm((rpad, half), BF16), vm((zn, rpad, half), BF16), vm((rpad, half), F32), vm((rpad, half), F32),
        vm((8, LANES), F32), vm((8, LANES), F32), vm((8, LANES), F32), vm((zn, 8, LANES), F32),
        dma((chunks,)), dma((chunks,)), dma((chunks,)), dma((chunks,)),
        dma((3, hn)), dma((3, hn)), dma((5,)), dma((5,)), dma((3, zn)), dma((3, zn)),
    ]
    spec = pl.BlockSpec(memory_space=pltpu.VMEM)
    gin, gval, gwbc, gwdt, gbias, galog = pl.pallas_call(
        functools.partial(kernel, zn, hn, bn, heads, split),
        out_shape=(
            jax.ShapeDtypeStruct((tokens, width), BF16),
            jax.ShapeDtypeStruct((tokens, values), BF16),
            jax.ShapeDtypeStruct((block, both), F32),
            jax.ShapeDtypeStruct((heads, width), F32),
            jax.ShapeDtypeStruct((1, heads), F32),
            jax.ShapeDtypeStruct((1, heads), F32),
        ),
        in_specs=[spec] * 7,
        out_specs=[spec] * 6,
        scratch_shapes=scratch,
        compiler_params=pltpu.CompilerParams(
            collective_id=0, has_side_effects=True, vmem_limit_bytes=56 << 20
        ),
    )(
        u_input.reshape(tokens, width), head_values.reshape(tokens, values), grad_output.reshape(tokens, values),
        w_bc, w_dt.T, dt_bias.reshape(1, heads), a_log.reshape(1, heads),
    )
    return (
        gin.reshape(1, tokens, width), gval.reshape(1, tokens, values), gwbc,
        gwdt.T, gbias.reshape(heads), galog.reshape(heads),
    )


def solution(mesh):
    sizes = (mesh.shape["tm"], mesh.shape["head"], mesh.shape["batch"])
    return jax.shard_map(
        functools.partial(on_device, sizes),
        mesh=mesh,
        in_specs=(
            P(("groups", "batch"), "tm", None),
            P(("groups", "batch"), "tm", "head"),
            P(("groups", "batch"), "tm", "head"),
            P(),
            P(None, "head"),
            P("head"),
            P("head"),
        ),
        out_specs=(
            P(("groups", "batch"), "tm", None),
            P(("groups", "batch"), "tm", "head"),
            P(("groups", "tm", "batch"), None),
            P("groups", "head"),
            P(("groups", "head")),
            P(("groups", "head")),
        ),
        check_vma=False,
    )
```

```python
import functools

import jax
import jax.numpy as jnp
from jax import lax
from jax.experimental import pallas as pl
from jax.experimental.pallas import tpu as pltpu
from jax.sharding import PartitionSpec as P

MESH = pl.DeviceIdType.MESH
F32 = jnp.float32
BF16 = jnp.bfloat16
LANES = 128
NT = (((1,), (1,)), ((), ()))
TN = (((0,), (0,)), ((), ()))


def dot(a, b, dims=(((1,), (0,)), ((), ()))):
    return lax.dot_general(a, b, dims, preferred_element_type=F32)


def dot_exact(a, b):
    return lax.dot_general(
        a, b, (((1,), (0,)), ((), ())),
        precision=lax.Precision.HIGHEST, preferred_element_type=F32,
    )


def kernel(
    zn, hn, bn, heads, split,
    u, x, g, wbc, wdt, bias, alog,
    gin, gval, gwbc, gwdt, gbias, galog,
    wpad, ut, rows, proj, l_t, l_sel, d_sel, xs, gs, own_f, own_b, gxi, st, dst, col_e, erows,
    direct, qd, gl, fin, gacc,
    sf, rf, sb, rb, wx, px, gpx, csend, crecv, plocal, zsend, zrecv, fsend, frecv,
    wsend, wrecv, wsum, wzsend, wzrecv, wfsend, wfrecv, smsend, smrecv, smzsend, smzrecv,
    f_ss, f_rs, b_ss, b_rs, h_ss, h_rs, c_ss, c_rs, z_ss, z_rs,
):
    z, hx, bt = lax.axis_index("tm"), lax.axis_index("head"), lax.axis_index("batch")
    tokens, width = u.shape
    pairs = heads // 2
    per = 2 if pairs % 2 == 0 else 1
    chunks = pairs // per
    stride = 2
    state = LANES
    rpad = wx.shape[1]
    half = width // bn
    lane = lax.broadcasted_iota(jnp.int32, (tokens, LANES), 1)
    lane1 = lax.broadcasted_iota(jnp.int32, (1, LANES), 1)
    low = lane < 64
    low1 = lane1 < 64

    barrier = pltpu.get_barrier_semaphore()
    for k in range(1, zn):
        pl.semaphore_signal(barrier, inc=1, device_id={"tm": lax.rem(z + k, zn)}, device_id_type=MESH)
    for k in range(1, hn):
        pl.semaphore_signal(barrier, inc=1, device_id={"head": lax.rem(hx + k, hn)}, device_id_type=MESH)
    for k in range(1, bn):
        pl.semaphore_signal(barrier, inc=1, device_id={"batch": lax.rem(bt + k, bn)}, device_id_type=MESH)

    wpad[...] = jnp.zeros_like(wpad)
    wpad[:heads, :] = wdt[...]
    rows[...] = jnp.zeros_like(rows)
    rows[0:1, :heads] = bias[...]
    rows[1:2, :heads] = alog[...]
    uu = u[...]
    proj[...] = dot(uu, wbc[...]).astype(BF16)
    pre = dot(uu, wpad[...], NT) + rows[0:1, :]
    delta = jnp.maximum(pre, 0.0) + jnp.log1p(jnp.exp(-jnp.abs(pre)))
    rate = -jnp.exp(rows[1:2, :])
    ti = lax.broadcasted_iota(jnp.int32, (tokens, tokens), 0)
    si = lax.broadcasted_iota(jnp.int32, (tokens, tokens), 1)
    log_decay = dot_exact((ti >= si).astype(F32), delta * rate)
    l_rows = log_decay.T
    for h in range(heads):
        l_t[h] = l_rows[h:h + 1, :]
    b_all, c_all = proj[:, :state], proj[:, state:]
    b_t = b_all.astype(F32).T.astype(BF16)
    c_t = c_all.astype(F32).T.astype(BF16)
    st[...] = jnp.where(ti <= si, dot(b_all, c_all, NT), 0.0)
    wx[hx] = wpad[:rpad, :]

    def pick(value, head):
        return jnp.sum(jnp.where(lane == head, value, 0.0), axis=1, keepdims=True)

    def summarize(p, carry):
        cols = pl.ds(pl.multiple_of(p * LANES, LANES), LANES)
        ls = jnp.where(low, pick(log_decay, 2 * p), pick(log_decay, 2 * p + 1))
        ds = jnp.where(low, pick(delta, 2 * p), pick(delta, 2 * p + 1))
        l_sel[p] = ls
        d_sel[p] = ds
        xv = (jnp.exp(ls[tokens - 1:tokens, :] - ls) * ds * x[:, cols].astype(F32)).astype(BF16)
        gv = (jnp.exp(ls) * g[:, cols].astype(F32)).astype(BF16)
        xs[p] = xv
        gs[p] = gv
        own_f[p] = dot(b_t, xv)
        own_b[p] = dot(c_t, gv)
        return carry

    lax.fori_loop(0, pairs, summarize, 0)

    dst[...] = jnp.zeros_like(dst)
    erows[...] = jnp.zeros_like(erows)
    direct[...] = jnp.zeros_like(direct)
    qd[...] = jnp.zeros_like(qd)
    gl[...] = jnp.zeros_like(gl)
    fin[...] = jnp.zeros_like(fin)
    gacc[...] = jnp.zeros_like(gacc)

    @pl.when(z == 0)
    def _():
        rf[...] = jnp.zeros_like(rf)

    @pl.when(z == zn - 1)
    def _():
        rb[...] = jnp.zeros_like(rb)

    pl.semaphore_wait(barrier, zn + hn + bn - 3)

    def head_copies(k):
        to = {"head": lax.rem(hx + k, hn)}
        return [
            pltpu.make_async_remote_copy(
                ref.at[hx], ref.at[hx], h_ss.at[i, k], h_rs.at[i, k], device_id=to, device_id_type=MESH
            )
            for i, ref in enumerate((wx, px, gpx))
        ]

    for k in range(1, hn):
        head_copies(k)[0].start()

    def chain_f(c):
        part = pl.ds(c * per, per)
        return pltpu.make_async_remote_copy(
            sf.at[part], rf.at[part], f_ss.at[c], f_rs.at[c],
            device_id={"tm": lax.rem(z + 1, zn)}, device_id_type=MESH,
        )

    def chain_b(c):
        part = pl.ds(c * per, per)
        return pltpu.make_async_remote_copy(
            sb.at[part], rb.at[part], b_ss.at[c], b_rs.at[c],
            device_id={"tm": lax.rem(z + zn - 1, zn)}, device_id_type=MESH,
        )

    def chain_step(c, first, last, make, own, send, recv):
        @pl.when((c >= 0) & (c < chunks))
        def _():
            @pl.when(jnp.logical_not(first))
            def _():
                make(c).wait_recv()

            @pl.when(jnp.logical_not(last))
            def _():
                for j in range(per):
                    p = c * per + j
                    total = jnp.exp(l_sel[p, tokens - 1:tokens, :])
                    send[p] = (total * recv[p].astype(F32) + own[p]).astype(BF16)
                make(c).start()

    lm = low.astype(F32).astype(BF16)

    def local_pair(p):
        cols = pl.ds(pl.multiple_of(p * LANES, LANES), LANES)
        gb = g[:, cols]
        xb = x[:, cols]
        sh = tokens // 2
        for s0 in (0, sh):
            t0 = s0
            gx = []
            gt = gb[t0:, :]
            sm = st[s0:s0 + sh, t0:]
            add = jnp.zeros((sh, tokens - t0), F32)
            zero = [jnp.zeros((1, t0), F32)] if t0 else []
            dr = direct[s0:s0 + sh, :]
            for j in range(2):
                keep = lm[s0:s0 + sh, :]
                xm = xb[s0:s0 + sh, :] * (keep if j == 0 else (1.0 - keep).astype(BF16))
                dm = dot(xm, gt, NT)
                lc = l_sel[p, s0:s0 + sh, 64 * j:64 * j + 1]
                dc = d_sel[p, s0:s0 + sh, 64 * j:64 * j + 1]
                lr = l_t[2 * p + j][:, t0:]
                decay = jnp.exp(jnp.minimum(lr - lc, 0.0))
                gx.append(dot((decay * sm).astype(BF16), gt))
                dmd = dm * decay
                add = add + dmd * dc
                w = dmd * sm
                dr = dr + jnp.where(lane[:sh] == 2 * p + j, jnp.sum(w, axis=1, keepdims=True), 0.0)
                ce = jnp.concatenate(zero + [jnp.sum(w * dc, axis=0, keepdims=True)], axis=1)
                col_e[2 * p + j] = ce if s0 == 0 else col_e[2 * p + j] + ce
            direct[s0:s0 + sh, :] = dr
            dst[s0:s0 + sh, t0:] += add
            gxi[p, s0:s0 + sh, :] = jnp.where(low[:sh], gx[0], gx[1])

    def mixed(i, carry):
        chain_step(i - z * stride, z == 0, z == zn - 1, chain_f, own_f, sf, rf)
        chain_step(i - (zn - 1 - z) * stride, z == zn - 1, z == 0, chain_b, own_b, sb, rb)

        @pl.when(i < pairs)
        def _():
            local_pair(i)

        return carry

    lax.fori_loop(0, max(pairs, (zn - 1) * stride + chunks), mixed, 0)

    def carried(p, carry):
        cols = pl.ds(pl.multiple_of(p * LANES, LANES), LANES)
        entering, leaving = rf[p], rb[p]
        ls, ds = l_sel[p], d_sel[p]
        last = ls[tokens - 1:tokens, :]
        car = jnp.exp(ls) * g[:, cols].astype(F32) * dot(c_all, entering)
        br = jnp.exp(last - ls) * dot(b_all, leaving)
        gval[:, cols] = (ds * (gxi[p] + br)).astype(BF16)
        q = x[:, cols].astype(F32) * br
        ends = jnp.exp(last) * jnp.sum(entering.astype(F32) * leaving.astype(F32), axis=0, keepdims=True)
        q_new, c_new, e_new = qd[...], gl[...], fin[...]
        for j in range(2):
            mine, mine1 = (low, low1) if j == 0 else (~low, ~low1)
            at, at1 = lane == 2 * p + j, lane1 == 2 * p + j
            q_new = q_new + jnp.where(at, jnp.sum(jnp.where(mine, q, 0.0), axis=1, keepdims=True), 0.0)
            c_new = c_new + jnp.where(at, jnp.sum(jnp.where(mine, car, 0.0), axis=1, keepdims=True), 0.0)
            e_new = e_new + jnp.where(at1, jnp.sum(jnp.where(mine1, ends, 0.0), axis=1, keepdims=True), 0.0)
        qd[...], gl[...], fin[...] = q_new, c_new, e_new
        gacc[:, :state] += dot(xs[p], leaving, NT)
        gacc[:, state:] += dot(gs[p], entering, NT)
        return carry

    lax.fori_loop(0, pairs, carried, 0)

    d_masked = jnp.where(ti <= si, dst[...], 0.0).astype(BF16)
    px[hx, :, :state] = (gacc[:, :state] + dot(d_masked, c_all)).astype(BF16)
    px[hx, :, state:] = (gacc[:, state:] + dot(d_masked, b_all, TN)).astype(BF16)
    for k in range(1, hn):
        head_copies(k)[1].start()

    q_all = qd[...]
    straight = direct[...] + q_all
    for h in range(heads):
        erows[h:h + 1, :] = col_e[h]
    g_log = gl[...] + erows[...].T - delta * straight
    tail = jnp.sum(delta * q_all, axis=0, keepdims=True) + fin[...]
    back = dot_exact((ti <= si).astype(F32), g_log) + tail
    g_delta = straight + rate * back
    g_pre = g_delta * jax.nn.sigmoid(pre)
    smsend[...] = jnp.zeros_like(smsend)
    smsend[0:1, :] = jnp.sum(g_pre, axis=0, keepdims=True)
    smsend[1:2, :] = jnp.sum(delta * back, axis=0, keepdims=True) * rate
    gpx[hx] = g_pre.T[:rpad, :].astype(BF16)
    for k in range(1, hn):
        head_copies(k)[2].start()
    wsend[...] = dot(gpx[hx], uu).astype(BF16)

    other = {"batch": lax.rem(bt + 1, bn)}

    def core_copy(i, src, to):
        return pltpu.make_async_remote_copy(src, to, c_ss.at[i], c_rs.at[i], device_id=other, device_id_type=MESH)

    core_w = core_copy(0, wsend, wrecv)
    core_s = core_copy(1, smsend, smrecv)
    core_p = core_copy(2, csend, crecv)
    core_f = core_copy(3, wfsend, wfrecv)
    core_w.start()
    core_s.start()

    def along(i, src, to, k):
        there = lax.rem(z + k, zn)
        return pltpu.make_async_remote_copy(
            src, to.at[z], z_ss.at[i, k], z_rs.at[i, k], device_id={"tm": there}, device_id_type=MESH
        )

    def each_z(body):
        def turn(k, carry):
            body(k)
            return carry

        lax.fori_loop(1, zn, turn, 0)

    def z_start_small(k):
        along(0, wzsend, wzrecv, k).start()
        along(1, smzsend, smzrecv, k).start()

    def z_start_large(k):
        along(2, zsend.at[lax.rem(z + k, zn)], zrecv, k).start()

    def z_wait_small(k):
        along(0, wzsend, wzrecv, k).wait()
        along(1, smzsend, smzrecv, k).wait()

    def z_wait_large(k):
        along(2, zsend.at[lax.rem(z + k, zn)], zrecv, k).wait()

    for k in range(width // 256):
        at = k * 256
        ut[at:at + 256, :] = u[:, at:at + 256].astype(F32).T.astype(BF16)

    core_w.wait()
    core_s.wait()
    wsum[...] = wsend[...].astype(F32) + wrecv[...].astype(F32)
    mine = pl.ds(pl.multiple_of(bt * half, LANES), half)
    theirs = pl.ds(pl.multiple_of(lax.rem(bt + 1, bn) * half, LANES), half)
    wz = wsum[:, mine].astype(BF16)
    wzsend[...] = wz
    wzrecv[z] = wz
    sz = smsend[...] + smrecv[...]
    smzsend[...] = sz
    smzrecv[z] = sz
    each_z(z_start_small)

    for k in range(1, hn):
        for copy in head_copies(k):
            copy.wait()
    gp = px[0].astype(F32)
    for k in range(1, hn):
        gp = gp + px[k].astype(F32)
    gp = gp.astype(BF16)
    wide = zrecv.shape[2]
    if split:
        piece = jnp.where(hx == 0, gp[:, :wide], gp[:, wide:])
    else:
        piece = gp
    block = zrecv.shape[1]
    local = dot(ut[...], piece)
    for k in range(zn * bn):
        plocal[k] = local[k * block:(k + 1) * block, :]
    for k in range(zn):
        csend[k] = plocal[k * bn + lax.rem(bt + 1, bn)].astype(BF16)
    core_p.start()

    core_p.wait()
    for k in range(zn):
        zsend[k] = (plocal[k * bn + bt] + crecv[k].astype(F32)).astype(BF16)
    zrecv[z] = zsend[z]
    each_z(z_start_large)

    gpa = gpx[...].reshape(hn * rpad, tokens).astype(F32).T.astype(BF16)
    wa = wx[...].reshape(hn * rpad, width)
    gin[...] = (dot(gp, wbc[...], NT) + dot(gpa, wa)).astype(BF16)

    each_z(z_wait_small)
    total_w = wzrecv[0].astype(F32)
    total_s = smzrecv[0]
    for k in range(1, zn):
        total_w = total_w + wzrecv[k].astype(F32)
        total_s = total_s + smzrecv[k]
    wfsend[...] = total_w
    core_f.start()
    gbias[...] = total_s[0:1, :heads]
    galog[...] = total_s[1:2, :heads]
    gwdt[:, mine] = total_w[:heads, :]

    each_z(z_wait_large)
    total = zrecv[0].astype(F32)
    for k in range(1, zn):
        total = total + zrecv[k].astype(F32)
    if split:
        fsend[...] = total
        final = pltpu.make_async_remote_copy(
            fsend, frecv, c_ss.at[4], c_rs.at[4], device_id={"head": lax.rem(hx + 1, hn)}, device_id_type=MESH
        )
        final.start()
        gwbc[:, pl.ds(pl.multiple_of(hx * wide, LANES), wide)] = total
        final.wait()
        gwbc[:, pl.ds(pl.multiple_of((1 - hx) * wide, LANES), wide)] = frecv[...]
    else:
        gwbc[...] = total
    core_f.wait()
    gwdt[:, theirs] = wfrecv[:heads, :]

    def drain(c, carry):
        @pl.when(z < zn - 1)
        def _():
            chain_f(c).wait_send()

        @pl.when(z > 0)
        def _():
            chain_b(c).wait_send()

        return carry

    lax.fori_loop(0, chunks, drain, 0)


def on_device(sizes, u_input, head_values, grad_output, w_bc, w_dt, dt_bias, a_log):
    zn, hn, bn = sizes
    seqs, tokens, width = u_input.shape
    assert seqs == 1 and bn == 2
    heads = w_dt.shape[1]
    values = head_values.shape[2]
    both = w_bc.shape[1]
    pairs = heads // 2
    assert values == heads * 64 and both == 2 * LANES and heads % 2 == 0
    split = hn == 2
    wide = both // 2 if split else both
    block = width // (zn * bn)
    rpad = -(-heads // 16) * 16
    half = width // bn
    chunks = pairs // 2 if pairs % 2 == 0 else pairs
    vm = pltpu.VMEM
    dma = pltpu.SemaphoreType.DMA
    scratch = [
        vm((LANES, width), BF16), vm((width, tokens), BF16), vm((8, LANES), F32), vm((tokens, both), BF16), vm((heads, 1, tokens), F32),
        vm((pairs, tokens, LANES), F32), vm((pairs, tokens, LANES), F32),
        vm((pairs, tokens, LANES), BF16), vm((pairs, tokens, LANES), BF16),
        vm((pairs, LANES, LANES), F32), vm((pairs, LANES, LANES), F32), vm((pairs, tokens, LANES), F32),
        vm((tokens, tokens), F32), vm((tokens, tokens), F32), vm((heads, 1, tokens), F32), vm((LANES, tokens), F32),
        vm((tokens, LANES), F32), vm((tokens, LANES), F32), vm((tokens, LANES), F32), vm((1, LANES), F32),
        vm((tokens, both), F32),
        vm((pairs, LANES, LANES), BF16), vm((pairs, LANES, LANES), BF16),
        vm((pairs, LANES, LANES), BF16), vm((pairs, LANES, LANES), BF16),
        vm((hn, rpad, width), BF16), vm((hn, tokens, both), BF16), vm((hn, rpad, tokens), BF16),
        vm((zn, block, wide), BF16), vm((zn, block, wide), BF16), vm((zn * bn, block, wide), F32),
        vm((zn, block, wide), BF16), vm((zn, block, wide), BF16), vm((block, wide), F32), vm((block, wide), F32),
        vm((rpad, width), BF16), vm((rpad, width), BF16), vm((rpad, width), F32),
        vm((rpad, half), BF16), vm((zn, rpad, half), BF16), vm((rpad, half), F32), vm((rpad, half), F32),
        vm((8, LANES), F32), vm((8, LANES), F32), vm((8, LANES), F32), vm((zn, 8, LANES), F32),
        dma((chunks,)), dma((chunks,)), dma((chunks,)), dma((chunks,)),
        dma((3, hn)), dma((3, hn)), dma((5,)), dma((5,)), dma((3, zn)), dma((3, zn)),
    ]
    spec = pl.BlockSpec(memory_space=pltpu.VMEM)
    gin, gval, gwbc, gwdt, gbias, galog = pl.pallas_call(
        functools.partial(kernel, zn, hn, bn, heads, split),
        out_shape=(
            jax.ShapeDtypeStruct((tokens, width), BF16),
            jax.ShapeDtypeStruct((tokens, values), BF16),
            jax.ShapeDtypeStruct((block, both), F32),
            jax.ShapeDtypeStruct((heads, width), F32),
            jax.ShapeDtypeStruct((1, heads), F32),
            jax.ShapeDtypeStruct((1, heads), F32),
        ),
        in_specs=[spec] * 7,
        out_specs=[spec] * 6,
        scratch_shapes=scratch,
        compiler_params=pltpu.CompilerParams(
            collective_id=0, has_side_effects=True, vmem_limit_bytes=56 << 20
        ),
    )(
        u_input.reshape(tokens, width), head_values.reshape(tokens, values), grad_output.reshape(tokens, values),
        w_bc, w_dt.T, dt_bias.reshape(1, heads), a_log.reshape(1, heads),
    )
    return (
        gin.reshape(1, tokens, width), gval.reshape(1, tokens, values), gwbc,
        gwdt.T, gbias.reshape(heads), galog.reshape(heads),
    )


def solution(mesh):
    sizes = (mesh.shape["tm"], mesh.shape["head"], mesh.shape["batch"])
    return jax.shard_map(
        functools.partial(on_device, sizes),
        mesh=mesh,
        in_specs=(
            P(("groups", "batch"), "tm", None),
            P(("groups", "batch"), "tm", "head"),
            P(("groups", "batch"), "tm", "head"),
            P(),
            P(None, "head"),
            P("head"),
            P("head"),
        ),
        out_specs=(
            P(("groups", "batch"), "tm", None),
            P(("groups", "batch"), "tm", "head"),
            P(("groups", "tm", "batch"), None),
            P("groups", "head"),
            P(("groups", "head")),
            P(("groups", "head")),
        ),
        check_vma=False,
    )
```

```python
import functools

import jax
import jax.numpy as jnp
from jax import lax
from jax.experimental import pallas as pl
from jax.experimental.pallas import tpu as pltpu
from jax.sharding import PartitionSpec as P

MESH = pl.DeviceIdType.MESH
F32 = jnp.float32
BF16 = jnp.bfloat16
LANES = 128
NT = (((1,), (1,)), ((), ()))
TN = (((0,), (0,)), ((), ()))


def dot(a, b, dims=(((1,), (0,)), ((), ()))):
    return lax.dot_general(a, b, dims, preferred_element_type=F32)


def dot_exact(a, b):
    return lax.dot_general(
        a, b, (((1,), (0,)), ((), ())),
        precision=lax.Precision.HIGHEST, preferred_element_type=F32,
    )


def kernel(
    zn, hn, bn, heads, split,
    u, x, g, wbc, wdt, bias, alog,
    gin, gval, gwbc, gwdt, gbias, galog,
    wpad, ut, rows, proj, l_t, l_sel, d_sel, xs, gs, own_f, own_b, gxi, st, dst, col_e, erows,
    direct, qd, gl, fin, gacc,
    sf, rf, sb, rb, wx, px, gpx, csend, crecv, plocal, zsend, zrecv, fsend, frecv,
    wsend, wrecv, wsum, wzsend, wzrecv, wfsend, wfrecv, smsend, smrecv, smzsend, smzrecv,
    f_ss, f_rs, b_ss, b_rs, h_ss, h_rs, c_ss, c_rs, z_ss, z_rs,
):
    z, hx, bt = lax.axis_index("tm"), lax.axis_index("head"), lax.axis_index("batch")
    tokens, width = u.shape
    pairs = heads // 2
    per = 2 if pairs % 2 == 0 else 1
    chunks = pairs // per
    stride = 2
    state = LANES
    rpad = wx.shape[1]
    half = width // bn

    def several(body, i, carry):
        for j in range(per):
            carry = body(i * per + j, carry)
        return carry

    lane = lax.broadcasted_iota(jnp.int32, (tokens, LANES), 1)
    lane1 = lax.broadcasted_iota(jnp.int32, (1, LANES), 1)
    low = lane < 64
    low1 = lane1 < 64

    barrier = pltpu.get_barrier_semaphore()
    for k in range(1, zn):
        pl.semaphore_signal(barrier, inc=1, device_id={"tm": lax.rem(z + k, zn)}, device_id_type=MESH)
    for k in range(1, hn):
        pl.semaphore_signal(barrier, inc=1, device_id={"head": lax.rem(hx + k, hn)}, device_id_type=MESH)
    for k in range(1, bn):
        pl.semaphore_signal(barrier, inc=1, device_id={"batch": lax.rem(bt + k, bn)}, device_id_type=MESH)

    wpad[...] = jnp.zeros_like(wpad)
    wpad[:heads, :] = wdt[...]
    rows[...] = jnp.zeros_like(rows)
    rows[0:1, :heads] = bias[...]
    rows[1:2, :heads] = alog[...]
    uu = u[...]
    proj[...] = dot(uu, wbc[...]).astype(BF16)
    pre = dot(uu, wpad[...], NT) + rows[0:1, :]
    delta = jnp.maximum(pre, 0.0) + jnp.log1p(jnp.exp(-jnp.abs(pre)))
    rate = -jnp.exp(rows[1:2, :])
    ti = lax.broadcasted_iota(jnp.int32, (tokens, tokens), 0)
    si = lax.broadcasted_iota(jnp.int32, (tokens, tokens), 1)
    log_decay = dot_exact((ti >= si).astype(F32), delta * rate)
    l_rows = log_decay.T
    for h in range(heads):
        l_t[h] = l_rows[h:h + 1, :]
    b_all, c_all = proj[:, :state], proj[:, state:]
    b_t = b_all.astype(F32).T.astype(BF16)
    c_t = c_all.astype(F32).T.astype(BF16)
    st[...] = jnp.where(ti <= si, dot(b_all, c_all, NT), 0.0)
    wx[hx] = wpad[:rpad, :]

    def pick(value, head):
        return jnp.sum(jnp.where(lane == head, value, 0.0), axis=1, keepdims=True)

    def summarize(p, carry):
        cols = pl.ds(pl.multiple_of(p * LANES, LANES), LANES)
        ls = jnp.where(low, pick(log_decay, 2 * p), pick(log_decay, 2 * p + 1))
        ds = jnp.where(low, pick(delta, 2 * p), pick(delta, 2 * p + 1))
        l_sel[p] = ls
        d_sel[p] = ds
        xv = (jnp.exp(ls[tokens - 1:tokens, :] - ls) * ds * x[:, cols].astype(F32)).astype(BF16)
        gv = (jnp.exp(ls) * g[:, cols].astype(F32)).astype(BF16)
        xs[p] = xv
        gs[p] = gv
        own_f[p] = dot(b_t, xv)
        own_b[p] = dot(c_t, gv)
        return carry

    lax.fori_loop(0, pairs // per, lambda i, carry: several(summarize, i, carry), 0)

    dst[...] = jnp.zeros_like(dst)
    erows[...] = jnp.zeros_like(erows)
    direct[...] = jnp.zeros_like(direct)
    qd[...] = jnp.zeros_like(qd)
    gl[...] = jnp.zeros_like(gl)
    fin[...] = jnp.zeros_like(fin)
    gacc[...] = jnp.zeros_like(gacc)

    @pl.when(z == 0)
    def _():
        rf[...] = jnp.zeros_like(rf)

    @pl.when(z == zn - 1)
    def _():
        rb[...] = jnp.zeros_like(rb)

    pl.semaphore_wait(barrier, zn + hn + bn - 3)

    def head_copies(k):
        to = {"head": lax.rem(hx + k, hn)}
        return [
            pltpu.make_async_remote_copy(
                ref.at[hx], ref.at[hx], h_ss.at[i, k], h_rs.at[i, k], device_id=to, device_id_type=MESH
            )
            for i, ref in enumerate((wx, px, gpx))
        ]

    for k in range(1, hn):
        head_copies(k)[0].start()

    def chain_f(c):
        part = pl.ds(c * per, per)
        return pltpu.make_async_remote_copy(
            sf.at[part], rf.at[part], f_ss.at[c], f_rs.at[c],
            device_id={"tm": lax.rem(z + 1, zn)}, device_id_type=MESH,
        )

    def chain_b(c):
        part = pl.ds(c * per, per)
        return pltpu.make_async_remote_copy(
            sb.at[part], rb.at[part], b_ss.at[c], b_rs.at[c],
            device_id={"tm": lax.rem(z + zn - 1, zn)}, device_id_type=MESH,
        )

    def chain_step(c, first, last, make, own, send, recv):
        @pl.when((c >= 0) & (c < chunks))
        def _():
            @pl.when(jnp.logical_not(first))
            def _():
                make(c).wait_recv()

            @pl.when(jnp.logical_not(last))
            def _():
                for j in range(per):
                    p = c * per + j
                    total = jnp.exp(l_sel[p, tokens - 1:tokens, :])
                    send[p] = (total * recv[p].astype(F32) + own[p]).astype(BF16)
                make(c).start()

    lm = low.astype(F32).astype(BF16)

    def local_pair(p):
        cols = pl.ds(pl.multiple_of(p * LANES, LANES), LANES)
        gb = g[:, cols]
        xb = x[:, cols]
        sh = tokens // 2
        for s0 in (0, sh):
            t0 = s0
            gx = []
            gt = gb[t0:, :]
            sm = st[s0:s0 + sh, t0:]
            add = jnp.zeros((sh, tokens - t0), F32)
            zero = [jnp.zeros((1, t0), F32)] if t0 else []
            dr = direct[s0:s0 + sh, :]
            for j in range(2):
                keep = lm[s0:s0 + sh, :]
                xm = xb[s0:s0 + sh, :] * (keep if j == 0 else (1.0 - keep).astype(BF16))
                dm = dot(xm, gt, NT)
                lc = l_sel[p, s0:s0 + sh, 64 * j:64 * j + 1]
                dc = d_sel[p, s0:s0 + sh, 64 * j:64 * j + 1]
                lr = l_t[2 * p + j][:, t0:]
                decay = jnp.exp(jnp.minimum(lr - lc, 0.0))
                gx.append(dot((decay * sm).astype(BF16), gt))
                dmd = dm * decay
                add = add + dmd * dc
                w = dmd * sm
                dr = dr + jnp.where(lane[:sh] == 2 * p + j, jnp.sum(w, axis=1, keepdims=True), 0.0)
                ce = jnp.concatenate(zero + [jnp.sum(w * dc, axis=0, keepdims=True)], axis=1)
                col_e[2 * p + j] = ce if s0 == 0 else col_e[2 * p + j] + ce
            direct[s0:s0 + sh, :] = dr
            dst[s0:s0 + sh, t0:] += add
            gxi[p, s0:s0 + sh, :] = jnp.where(low[:sh], gx[0], gx[1])

    def mixed(i, carry):
        chain_step(i - z * stride, z == 0, z == zn - 1, chain_f, own_f, sf, rf)
        chain_step(i - (zn - 1 - z) * stride, z == zn - 1, z == 0, chain_b, own_b, sb, rb)

        @pl.when(i < pairs)
        def _():
            local_pair(i)

        return carry

    lax.fori_loop(0, max(pairs, (zn - 1) * stride + chunks), mixed, 0)

    def carried(p, carry):
        cols = pl.ds(pl.multiple_of(p * LANES, LANES), LANES)
        entering, leaving = rf[p], rb[p]
        ls, ds = l_sel[p], d_sel[p]
        last = ls[tokens - 1:tokens, :]
        car = jnp.exp(ls) * g[:, cols].astype(F32) * dot(c_all, entering)
        br = jnp.exp(last - ls) * dot(b_all, leaving)
        gval[:, cols] = (ds * (gxi[p] + br)).astype(BF16)
        q = x[:, cols].astype(F32) * br
        ends = jnp.exp(last) * jnp.sum(entering.astype(F32) * leaving.astype(F32), axis=0, keepdims=True)
        q_new, c_new, e_new = qd[...], gl[...], fin[...]
        for j in range(2):
            mine, mine1 = (low, low1) if j == 0 else (~low, ~low1)
            at, at1 = lane == 2 * p + j, lane1 == 2 * p + j
            q_new = q_new + jnp.where(at, jnp.sum(jnp.where(mine, q, 0.0), axis=1, keepdims=True), 0.0)
            c_new = c_new + jnp.where(at, jnp.sum(jnp.where(mine, car, 0.0), axis=1, keepdims=True), 0.0)
            e_new = e_new + jnp.where(at1, jnp.sum(jnp.where(mine1, ends, 0.0), axis=1, keepdims=True), 0.0)
        qd[...], gl[...], fin[...] = q_new, c_new, e_new
        gacc[:, :state] += dot(xs[p], leaving, NT)
        gacc[:, state:] += dot(gs[p], entering, NT)
        return carry

    lax.fori_loop(0, pairs // per, lambda i, carry: several(carried, i, carry), 0)

    d_masked = jnp.where(ti <= si, dst[...], 0.0).astype(BF16)
    px[hx, :, :state] = (gacc[:, :state] + dot(d_masked, c_all)).astype(BF16)
    px[hx, :, state:] = (gacc[:, state:] + dot(d_masked, b_all, TN)).astype(BF16)
    for k in range(1, hn):
        head_copies(k)[1].start()

    q_all = qd[...]
    straight = direct[...] + q_all
    for h in range(heads):
        erows[h:h + 1, :] = col_e[h]
    g_log = gl[...] + erows[...].T - delta * straight
    tail = jnp.sum(delta * q_all, axis=0, keepdims=True) + fin[...]
    back = dot_exact((ti <= si).astype(F32), g_log) + tail
    g_delta = straight + rate * back
    g_pre = g_delta * jax.nn.sigmoid(pre)
    smsend[...] = jnp.zeros_like(smsend)
    smsend[0:1, :] = jnp.sum(g_pre, axis=0, keepdims=True)
    smsend[1:2, :] = jnp.sum(delta * back, axis=0, keepdims=True) * rate
    gpx[hx] = g_pre.T[:rpad, :].astype(BF16)
    for k in range(1, hn):
        head_copies(k)[2].start()
    wsend[...] = dot(gpx[hx], uu).astype(BF16)

    other = {"batch": lax.rem(bt + 1, bn)}

    def core_copy(i, src, to):
        return pltpu.make_async_remote_copy(src, to, c_ss.at[i], c_rs.at[i], device_id=other, device_id_type=MESH)

    core_w = core_copy(0, wsend, wrecv)
    core_s = core_copy(1, smsend, smrecv)
    core_p = core_copy(2, csend, crecv)
    core_f = core_copy(3, wfsend, wfrecv)
    core_w.start()
    core_s.start()

    def along(i, src, to, k):
        there = lax.rem(z + k, zn)
        return pltpu.make_async_remote_copy(
            src, to.at[z], z_ss.at[i, k], z_rs.at[i, k], device_id={"tm": there}, device_id_type=MESH
        )

    def each_z(body):
        def turn(k, carry):
            body(k)
            return carry

        lax.fori_loop(1, zn, turn, 0)

    def z_start_small(k):
        along(0, wzsend, wzrecv, k).start()
        along(1, smzsend, smzrecv, k).start()

    def z_start_large(k):
        along(2, zsend.at[lax.rem(z + k, zn)], zrecv, k).start()

    def z_wait_small(k):
        along(0, wzsend, wzrecv, k).wait()
        along(1, smzsend, smzrecv, k).wait()

    def z_wait_large(k):
        along(2, zsend.at[lax.rem(z + k, zn)], zrecv, k).wait()

    for k in range(width // 256):
        at = k * 256
        ut[at:at + 256, :] = u[:, at:at + 256].astype(F32).T.astype(BF16)

    core_w.wait()
    core_s.wait()
    wsum[...] = wsend[...].astype(F32) + wrecv[...].astype(F32)
    mine = pl.ds(pl.multiple_of(bt * half, LANES), half)
    theirs = pl.ds(pl.multiple_of(lax.rem(bt + 1, bn) * half, LANES), half)
    wz = wsum[:, mine].astype(BF16)
    wzsend[...] = wz
    wzrecv[z] = wz
    sz = smsend[...] + smrecv[...]
    smzsend[...] = sz
    smzrecv[z] = sz
    each_z(z_start_small)

    for k in range(1, hn):
        for copy in head_copies(k):
            copy.wait()
    gp = px[0].astype(F32)
    for k in range(1, hn):
        gp = gp + px[k].astype(F32)
    gp = gp.astype(BF16)
    wide = zrecv.shape[2]
    if split:
        piece = jnp.where(hx == 0, gp[:, :wide], gp[:, wide:])
    else:
        piece = gp
    block = zrecv.shape[1]
    local = dot(ut[...], piece)
    for k in range(zn * bn):
        plocal[k] = local[k * block:(k + 1) * block, :]
    for k in range(zn):
        csend[k] = plocal[k * bn + lax.rem(bt + 1, bn)].astype(BF16)
    core_p.start()

    core_p.wait()
    for k in range(zn):
        zsend[k] = (plocal[k * bn + bt] + crecv[k].astype(F32)).astype(BF16)
    zrecv[z] = zsend[z]
    each_z(z_start_large)

    gpa = gpx[...].reshape(hn * rpad, tokens).astype(F32).T.astype(BF16)
    wa = wx[...].reshape(hn * rpad, width)
    gin[...] = (dot(gp, wbc[...], NT) + dot(gpa, wa)).astype(BF16)

    each_z(z_wait_small)
    total_w = wzrecv[0].astype(F32)
    total_s = smzrecv[0]
    for k in range(1, zn):
        total_w = total_w + wzrecv[k].astype(F32)
        total_s = total_s + smzrecv[k]
    wfsend[...] = total_w
    core_f.start()
    gbias[...] = total_s[0:1, :heads]
    galog[...] = total_s[1:2, :heads]
    gwdt[:, mine] = total_w[:heads, :]

    each_z(z_wait_large)
    total = zrecv[0].astype(F32)
    for k in range(1, zn):
        total = total + zrecv[k].astype(F32)
    if split:
        fsend[...] = total
        final = pltpu.make_async_remote_copy(
            fsend, frecv, c_ss.at[4], c_rs.at[4], device_id={"head": lax.rem(hx + 1, hn)}, device_id_type=MESH
        )
        final.start()
        gwbc[:, pl.ds(pl.multiple_of(hx * wide, LANES), wide)] = total
        final.wait()
        gwbc[:, pl.ds(pl.multiple_of((1 - hx) * wide, LANES), wide)] = frecv[...]
    else:
        gwbc[...] = total
    core_f.wait()
    gwdt[:, theirs] = wfrecv[:heads, :]

    def drain(c, carry):
        @pl.when(z < zn - 1)
        def _():
            chain_f(c).wait_send()

        @pl.when(z > 0)
        def _():
            chain_b(c).wait_send()

        return carry

    lax.fori_loop(0, chunks, drain, 0)


def on_device(sizes, u_input, head_values, grad_output, w_bc, w_dt, dt_bias, a_log):
    zn, hn, bn = sizes
    seqs, tokens, width = u_input.shape
    assert seqs == 1 and bn == 2
    heads = w_dt.shape[1]
    values = head_values.shape[2]
    both = w_bc.shape[1]
    pairs = heads // 2
    assert values == heads * 64 and both == 2 * LANES and heads % 2 == 0
    split = hn == 2
    wide = both // 2 if split else both
    block = width // (zn * bn)
    rpad = -(-heads // 16) * 16
    half = width // bn
    chunks = pairs // 2 if pairs % 2 == 0 else pairs
    vm = pltpu.VMEM
    dma = pltpu.SemaphoreType.DMA
    scratch = [
        vm((LANES, width), BF16), vm((width, tokens), BF16), vm((8, LANES), F32), vm((tokens, both), BF16), vm((heads, 1, tokens), F32),
        vm((pairs, tokens, LANES), F32), vm((pairs, tokens, LANES), F32),
        vm((pairs, tokens, LANES), BF16), vm((pairs, tokens, LANES), BF16),
        vm((pairs, LANES, LANES), F32), vm((pairs, LANES, LANES), F32), vm((pairs, tokens, LANES), F32),
        vm((tokens, tokens), F32), vm((tokens, tokens), F32), vm((heads, 1, tokens), F32), vm((LANES, tokens), F32),
        vm((tokens, LANES), F32), vm((tokens, LANES), F32), vm((tokens, LANES), F32), vm((1, LANES), F32),
        vm((tokens, both), F32),
        vm((pairs, LANES, LANES), BF16), vm((pairs, LANES, LANES), BF16),
        vm((pairs, LANES, LANES), BF16), vm((pairs, LANES, LANES), BF16),
        vm((hn, rpad, width), BF16), vm((hn, tokens, both), BF16), vm((hn, rpad, tokens), BF16),
        vm((zn, block, wide), BF16), vm((zn, block, wide), BF16), vm((zn * bn, block, wide), F32),
        vm((zn, block, wide), BF16), vm((zn, block, wide), BF16), vm((block, wide), F32), vm((block, wide), F32),
        vm((rpad, width), BF16), vm((rpad, width), BF16), vm((rpad, width), F32),
        vm((rpad, half), BF16), vm((zn, rpad, half), BF16), vm((rpad, half), F32), vm((rpad, half), F32),
        vm((8, LANES), F32), vm((8, LANES), F32), vm((8, LANES), F32), vm((zn, 8, LANES), F32),
        dma((chunks,)), dma((chunks,)), dma((chunks,)), dma((chunks,)),
        dma((3, hn)), dma((3, hn)), dma((5,)), dma((5,)), dma((3, zn)), dma((3, zn)),
    ]
    spec = pl.BlockSpec(memory_space=pltpu.VMEM)
    gin, gval, gwbc, gwdt, gbias, galog = pl.pallas_call(
        functools.partial(kernel, zn, hn, bn, heads, split),
        out_shape=(
            jax.ShapeDtypeStruct((tokens, width), BF16),
            jax.ShapeDtypeStruct((tokens, values), BF16),
            jax.ShapeDtypeStruct((block, both), F32),
            jax.ShapeDtypeStruct((heads, width), F32),
            jax.ShapeDtypeStruct((1, heads), F32),
            jax.ShapeDtypeStruct((1, heads), F32),
        ),
        in_specs=[spec] * 7,
        out_specs=[spec] * 6,
        scratch_shapes=scratch,
        compiler_params=pltpu.CompilerParams(
            collective_id=0, has_side_effects=True, vmem_limit_bytes=56 << 20
        ),
    )(
        u_input.reshape(tokens, width), head_values.reshape(tokens, values), grad_output.reshape(tokens, values),
        w_bc, w_dt.T, dt_bias.reshape(1, heads), a_log.reshape(1, heads),
    )
    return (
        gin.reshape(1, tokens, width), gval.reshape(1, tokens, values), gwbc,
        gwdt.T, gbias.reshape(heads), galog.reshape(heads),
    )


def solution(mesh):
    sizes = (mesh.shape["tm"], mesh.shape["head"], mesh.shape["batch"])
    return jax.shard_map(
        functools.partial(on_device, sizes),
        mesh=mesh,
        in_specs=(
            P(("groups", "batch"), "tm", None),
            P(("groups", "batch"), "tm", "head"),
            P(("groups", "batch"), "tm", "head"),
            P(),
            P(None, "head"),
            P("head"),
            P("head"),
        ),
        out_specs=(
            P(("groups", "batch"), "tm", None),
            P(("groups", "batch"), "tm", "head"),
            P(("groups", "tm", "batch"), None),
            P("groups", "head"),
            P(("groups", "head")),
            P(("groups", "head")),
        ),
        check_vma=False,
    )
```
